32 devices in a mesh: rows: 8 (over y, x, core), probe: 4 (over z).
Axes of the slice: x: 2, y: 2, z: 4, core: 2. Of those that a mesh axis runs over, the one named last changes fastest.
Arguments:
- points: float32 [64, 3, 128], P('rows'), may hold values from 0 to 1
- observations: float32 [64, 128], P('rows'), may hold values from -6 to 6
- probes: float32 [64, 64, 128], P('rows', 'probe'), may hold values from -150 to 150
- neighbours: int32 [64, 3], P('rows'), may hold values from 0 to 63, as said below
- block_position: int32 [64], P('rows'), may hold values from 0 to 63, as said below
Outputs:
- whitened: float32 [64, 128], P('rows')
- block_terms: float32 [64], P('rows')
- tridiagonal: float32 [64, 3], P('probe')
- remainder: float32 [64, 64, 128], P('rows', 'probe')
The draws below stay inside these ranges and needn't reach their ends.
Inputs may be any that keep to these rules, and one draw needn't show every extreme that they name: block_position is a permutation of the block ids; the block with id i sits at position block_position[i], on index block_position[i] // 8 of rows. neighbours[b] lists three block ids, which may repeat and may name the block at b itself. Over the 24 references of the blocks of one index of rows, the positions of the named blocks fall at most 6 times on the blocks of any one index of rows, and exactly 6 times on those of some index, for every index.
All inputs are finite; a program needn't handle non-finite values.
Results may differ from the reference program's by a relative error of at most 0.0003.
Values sent between devices are 32-bit elements; how exact they have to be, the bound alone decides.
A program may use at most 64 MiB of HBM per device.

```python
import math
import jax
import jax.numpy as jnp
from jax import lax

BS = 128
BLK_DEV = 8
PROBES = 64
NB = 64
CAP = 6


def neighbour_layout(key):
    base_key = jax.random.fold_in(key, 7)
    devices = NB // BLK_DEV
    references = 3 * BLK_DEV
    slot_count = devices * CAP

    def per_device(device):
        dev_key = jax.random.fold_in(base_key, device)
        key_one, key_two, key_three, key_four = jax.random.split(dev_key, 4)
        forced = jax.random.randint(key_one, (), 0, devices)
        slot_ids = jnp.arange(slot_count, dtype=jnp.int32)
        slot_owner = slot_ids // CAP
        distance = jnp.abs(slot_owner - device)
        jitter = jax.random.randint(key_two, (slot_count,), 0, 1024)
        scores = jitter * 4096 + slot_ids - distance * (1 << 20) + jnp.where(slot_owner == forced, 1 << 28, 0)
        top_scores, chosen = lax.top_k(scores, references)
        shuffle = jax.random.permutation(key_three, references)
        owners = (chosen // CAP)[shuffle]
        local_rows = jax.random.randint(key_four, (references,), 0, BLK_DEV)
        return owners * BLK_DEV + local_rows
    positions = jax.vmap(per_device)(jnp.arange(devices, dtype=jnp.int32))
    placement_perm = jax.random.permutation(jax.random.fold_in(base_key, 100003), NB).astype(jnp.int32)
    id_at = jnp.argsort(placement_perm).astype(jnp.int32)
    near_ids = id_at[positions.reshape(NB, 3)]
    return (near_ids.astype(jnp.int32), placement_perm)


def draw_neighbours(key, part):
    return neighbour_layout(key)[0]


def draw_block_position(key, part):
    return neighbour_layout(key)[1]


def draw_probes(key, part):
    key_one, key_two, key_three = jax.random.split(jax.random.fold_in(key, 11), 3)
    position_trend = jnp.arange(NB, dtype=jnp.float32) / NB
    roughness = jax.random.uniform(key_two, (NB,), jnp.float32, -0.7, 0.7)
    column = jax.random.uniform(key_three, (PROBES,), jnp.float32, -1.1, 1.1)
    base_draw = jnp.clip(jax.random.normal(key_one, (NB, PROBES, BS), jnp.float32), -4.0, 4.0)
    growth = 1.1
    scaling = jnp.exp(growth * position_trend + roughness)[:, None, None] * jnp.exp(column)[None, :, None]
    return base_draw * scaling


def block_levels(own_key, extent, cuts, least, top_value):
    factor_of, own = 1.0, jax.random.fold_in(own_key, 6)
    for dim, blocks in cuts:
        steps = jnp.exp(jax.random.uniform(jax.random.fold_in(own, dim), (blocks,), jnp.float32, least / len(cuts), top_value / len(cuts)))
        factor_of = factor_of * jnp.repeat(steps, extent[dim] // blocks).reshape([-1 if axis == dim else 1 for axis in range(len(extent))])
    return factor_of


def gaussian(key, dims, scale, most, shards=(), kind=jnp.bfloat16):
    result = scale * jax.random.normal(key, dims, jnp.float32)
    if shards:
        result = result * block_levels(key, dims, shards, -0.22, 0.18)
    return jnp.clip(result, -most, most).astype(kind)


def setup_inputs(seed: int = 0) -> dict:
    key_list = jax.random.split(jax.random.key(seed), 6)
    points = jnp.clip(1.0 * jax.random.uniform(key_list[0], (NB, 3, BS), jnp.float32) ** block_levels(key_list[0], (NB, 3, BS), ((0, 8),), -0.2, 0.2), 0.0, 1.0)
    observations = gaussian(key_list[1], (NB, BS), 1.0, 6.0, ((0, 8),), jnp.float32)
    probes = draw_probes(jax.random.fold_in(key_list[5], 71), 0)
    neighbours = draw_neighbours(jax.random.fold_in(key_list[5], 71), 0)
    block_position = draw_block_position(jax.random.fold_in(key_list[5], 71), 0)
    return {"points": points, "observations": observations, "probes": probes, "neighbours": neighbours, "block_position": block_position}


length_scale = 0.3
nugget = 0.25
epsilon = 1e-06
highest = lax.Precision.HIGHEST

def factor_block(inputs):
    near_points, own_points, near_values, own_values = inputs
    block_size = own_points.shape[-1]
    point_set = jnp.concatenate([jnp.transpose(near_points, (1, 0, 2)).reshape(3, 3 * block_size), own_points], axis=1)
    offsets = point_set[:, :, None] - point_set[:, None, :]
    dist_sq = lax.optimization_barrier(jnp.sum(offsets * offsets, axis=0))
    matrix_order = 4 * block_size
    identity = jnp.eye(matrix_order, dtype=jnp.float32)
    kernel = 1.0 / (1.0 + dist_sq / (length_scale * length_scale)) + nugget * identity
    factor_low = jnp.linalg.cholesky(kernel)
    inverse = jax.scipy.linalg.solve_triangular(factor_low, identity, lower=True)
    conditioner = inverse[3 * block_size:]
    values = jnp.concatenate([near_values.reshape(3 * block_size), own_values])
    whitened = jnp.dot(conditioner, values, precision=highest)
    log_diag = jnp.sum(jnp.log(jnp.diagonal(factor_low)[3 * block_size:]))
    log_term = (-0.5 * jnp.sum(whitened * whitened) - log_diag) / block_size - 0.5 * math.log(2.0 * math.pi)
    return (conditioner, whitened, log_term)

def reference(points, observations, probes, neighbours, block_position):
    near_rows = block_position[neighbours]
    conditioner, whitened, block_terms = lax.map(factor_block, (points[near_rows], points, observations[near_rows], observations))
    cond_four = conditioner.reshape(NB, BS, 4, BS)
    flat_rows = near_rows.reshape(NB * 3)
    cells = NB * BS

    def apply_operator(vector):
        stacked = jnp.concatenate([vector[near_rows], vector[:, None]], axis=1)
        projected = jnp.einsum('bjpm,bkjm->bpk', stacked, cond_four, precision=highest)
        spread = jnp.einsum('bpk,bkjm->bjpm', projected, cond_four, precision=highest)
        moved = jnp.zeros_like(vector).at[flat_rows].add(spread[:, :3].reshape(NB * 3, PROBES, BS))
        return spread[:, 3] + moved

    def mean_inner(left, right):
        return lax.optimization_barrier(jnp.sum(left * right, axis=(0, 2))) / cells
    basis_one = probes / jnp.sqrt(mean_inner(probes, probes) + epsilon)[None, :, None]
    image_one = apply_operator(basis_one)
    alpha_one = mean_inner(basis_one, image_one)
    residue = image_one - alpha_one[None, :, None] * basis_one
    beta_one = jnp.sqrt(mean_inner(residue, residue) + epsilon)
    basis_two = residue / beta_one[None, :, None]
    image_two = apply_operator(basis_two)
    alpha_two = mean_inner(basis_two, image_two)
    remainder = image_two - alpha_two[None, :, None] * basis_two - beta_one[None, :, None] * basis_one
    tridiagonal = jnp.stack([alpha_one, beta_one, alpha_two], axis=1)
    return (whitened, block_terms, tridiagonal, remainder)
```

```python
import math

import jax
import jax.numpy as jnp
from jax import lax
from jax.experimental import pallas as pl
from jax.experimental.pallas import tpu as pltpu
from jax.sharding import PartitionSpec as P

length_scale = 0.3
nugget = 0.25
epsilon = 1e-06
highest = lax.Precision.HIGHEST
chunk = 8
width = 4


def dot(left, right):
    return jnp.dot(left, right, precision=highest, preferred_element_type=jnp.float32)


def dot_nt(left, right):
    return lax.dot_general(
        left, right, (((1,), (1,)), ((), ())), precision=highest,
        preferred_element_type=jnp.float32,
    )


def pivot_inverse(rows, e):
    rows = list(rows)
    e = [list(r) for r in e]
    for k in range(width):
        inv = 1.0 / e[k][k]
        rows[k] = rows[k] * inv
        for n in range(k + 1, width):
            e[k][n] = e[k][n] * inv
        for m in range(width):
            if m != k:
                f = e[m][k]
                rows[m] = rows[m] - f * rows[k]
                for n in range(k + 1, width):
                    e[m][n] = e[m][n] - f * e[k][n]
    return rows


def pivot_factor(rows, e):
    e = [list(r) for r in e]
    y = list(rows)
    inv = []
    product = None
    for k in range(width):
        d = e[k][k]
        s = lax.rsqrt(d)
        s = s * (1.5 - 0.5 * d * s * s)
        inv.append(s)
        product = s if product is None else product * s
        y[k] = y[k] * s
        for m in range(k + 1, width):
            e[m][k] = e[m][k] * s
        for m in range(k + 1, width):
            y[m] = y[m] - e[m][k] * y[k]
            for n in range(k + 1, m + 1):
                e[m][n] = e[m][n] - e[m][k] * e[n][k]
    r = list(y)
    for k in reversed(range(width)):
        for m in range(k + 1, width):
            r[k] = r[k] - e[m][k] * r[m]
        r[k] = r[k] * inv[k]
    return y, r, jnp.log(product)


def sweep(mats, factor):
    count = len(mats[0])
    shape = mats[0][0].shape
    lane = lax.broadcasted_iota(jnp.int32, shape, 1)
    sub = lax.broadcasted_iota(jnp.int32, shape, 0)

    def full(x):
        return jnp.broadcast_to(x, shape)

    def step(t, carry):
        mats, logs = carry
        mats = [list(m) for m in mats]
        logs = list(logs)
        for o in range(0, chunk, width):
            picked = (lane >= o) & (lane < o + width)
            for b in range(len(mats)):
                chunks = mats[b]
                top = chunks[0]
                cols = [full(top[:, o + k : o + k + 1]) for k in range(width)]
                rows = [full(top[o + k : o + k + 1, :]) for k in range(width)]
                e = [[full(cols[k][o + m : o + m + 1, :]) for k in range(width)] for m in range(width)]
                rows = [
                    jnp.where(lane == o + k, 1.0, jnp.where(picked, 0.0, rows[k]))
                    for k in range(width)
                ]
                if factor:
                    kept, r, term = pivot_factor(rows, e)
                    logs[b] = logs[b] + term
                else:
                    r = pivot_inverse(rows, e)
                    kept = r
                for p in range(count):
                    old = chunks[p]
                    if p:
                        cols = [full(old[:, o + k : o + k + 1]) for k in range(width)]
                    new = jnp.where(picked, 0.0, old)
                    for k in range(width):
                        new = new - cols[k] * r[k]
                    if p == 0:
                        if factor:
                            new = jnp.where(sub >= o + width, new, old)
                        for k in range(width):
                            new = jnp.where(sub == o + k, kept[k], new)
                    elif factor:
                        new = jnp.where(t + p < count, new, old)
                    chunks[p] = new
        turned = []
        for chunks in mats:
            chunks = [pltpu.roll(c, shape[1] - chunk, 1) for c in chunks]
            turned.append(tuple(chunks[1:] + chunks[:1]))
        return tuple(turned), tuple(logs)

    zero = jnp.zeros(shape, jnp.float32)
    return lax.fori_loop(0, count, step, (mats, tuple(zero for _ in mats)))


def factor_kernel(rows_ref, cols_ref, vals_ref, g_ref, w_ref, t_ref, a_ref):
    nb = rows_ref.shape[0]
    bs = g_ref.shape[1]

    def part(i):
        return slice(i * bs, (i + 1) * bs)

    def load(j):
        return tuple(
            tuple(
                a_ref[b, j * bs + i * chunk : j * bs + (i + 1) * chunk, part(j)]
                for i in range(bs // chunk)
            )
            for b in range(nb)
        )

    same = lax.broadcasted_iota(jnp.int32, (bs, bs), 0) == lax.broadcasted_iota(
        jnp.int32, (bs, bs), 1
    )
    below = lax.broadcasted_iota(jnp.int32, (bs, bs), 0) >= lax.broadcasted_iota(
        jnp.int32, (bs, bs), 1
    )
    for b in range(nb):
        for i in range(4):
            for k in range(i + 1):
                dist_sq = None
                for c in range(3):
                    off = cols_ref[b, part(i), c : c + 1] - rows_ref[b, c : c + 1, part(k)]
                    dist_sq = off * off if dist_sq is None else dist_sq + off * off
                value = 1.0 / (1.0 + dist_sq * (1.0 / (length_scale * length_scale)))
                if i == k:
                    value = value + jnp.where(same, nugget, 0.0)
                a_ref[b, part(i), part(k)] = value
    for j in range(3):
        inverse, _ = sweep(load(j), False)
        for b in range(nb):
            p = jnp.concatenate(inverse[b], axis=0)
            rest = a_ref[b, (j + 1) * bs :, part(j)]
            scaled = dot(rest, p)
            for i in range(j + 1, 4):
                row = scaled[(i - j - 1) * bs : (i - j) * bs]
                a_ref[b, part(i), (j + 1) * bs : (i + 1) * bs] -= dot_nt(
                    row, rest[: (i - j) * bs]
                )
            a_ref[b, (j + 1) * bs :, part(j)] = scaled
    low, logs = sweep(load(3), True)
    for b in range(nb):
        low_inv = jnp.where(below, jnp.concatenate(low[b], axis=0), 0.0)
        x2 = a_ref[b, part(3), part(2)]
        x1 = a_ref[b, part(3), part(1)] - dot(x2, a_ref[b, part(2), part(1)])
        x0 = (
            a_ref[b, part(3), part(0)]
            - dot(x1, a_ref[b, part(1), part(0)])
            - dot(x2, a_ref[b, part(2), part(0)])
        )
        g_ref[b, :, part(3)] = low_inv
        for i, x in enumerate((x0, x1, x2)):
            g_ref[b, :, part(i)] = -dot(low_inv, x)
        w = dot_nt(vals_ref[b], g_ref[b])
        w_ref[b] = w
        square = jnp.sum(w[:1] * w[:1], axis=1, keepdims=True)
        t_ref[b] = (logs[b] - 0.5 * square) * (1.0 / bs) - 0.5 * math.log(2.0 * math.pi)


def factor_blocks(points, values):
    nb, dims, order = points.shape
    bs = order // 4
    rows = jnp.pad(points, ((0, 0), (0, chunk - dims), (0, 0)))
    cols = jnp.swapaxes(points, 1, 2)
    vals = jnp.broadcast_to(values[:, None], (nb, chunk, order))
    g, w, t = pl.pallas_call(
        factor_kernel,
        out_shape=(
            jax.ShapeDtypeStruct((nb, bs, order), jnp.float32),
            jax.ShapeDtypeStruct((nb, chunk, bs), jnp.float32),
            jax.ShapeDtypeStruct((nb, chunk, bs), jnp.float32),
        ),
        scratch_shapes=[pltpu.VMEM((nb, order, order), jnp.float32)],
    )(rows, cols, vals)
    return g, w[:, 0], t[:, 0, 0]


def local_inner(left, right):
    return jnp.sum(left * right, axis=(0, 2))


def body(points, observations, probes, neighbours, block_position):
    row_count = lax.axis_size("rows")
    blocks = points.shape[0]
    block_size = points.shape[2]
    probe_cols = probes.shape[1]
    cells = blocks * row_count * block_size
    references = 3 * blocks
    capacity = max(2, 6 * blocks // row_count)
    slot_count = row_count * capacity
    whole_position = lax.all_gather(block_position, "rows", axis=0, tiled=True)
    all_blocks = whole_position.shape[0]
    block_ids = jnp.arange(all_blocks, dtype=jnp.int32)
    near_ids = neighbours.reshape(references)
    near_rows = jnp.sum(
        jnp.where(near_ids[:, None] == block_ids[None, :], whole_position[None, :], 0), axis=1
    )
    coord_rows = points.reshape(blocks, 3 * block_size)
    owners = near_rows // blocks
    local_rows = near_rows % blocks
    ref_index = jnp.arange(references, dtype=jnp.int32)
    earlier = (owners[:, None] == owners[None, :]) & (ref_index[:, None] > ref_index[None, :])
    slot_index = owners * capacity + jnp.sum(earlier.astype(jnp.int32), axis=1)
    slot_hits = slot_index[:, None] == jnp.arange(slot_count, dtype=jnp.int32)[None, :]
    to_slot = slot_hits.astype(jnp.float32)
    wanted = jnp.sum(jnp.where(slot_hits, local_rows[:, None] + 1, 0), axis=0) - 1
    requested = lax.all_to_all(
        wanted.reshape(row_count, capacity), "rows", split_axis=0, concat_axis=0, tiled=True
    ).reshape(slot_count)
    picked = (requested[:, None] == jnp.arange(blocks, dtype=jnp.int32)[None, :]).astype(
        jnp.float32
    )

    def select_rows(source):
        return jnp.dot(picked, source, precision=highest).reshape(
            row_count, capacity, source.shape[1]
        )

    def to_refs(incoming):
        return jnp.dot(to_slot, incoming.reshape(slot_count, incoming.shape[2]), precision=highest)

    def fetch_rows(source):
        return to_refs(
            lax.all_to_all(select_rows(source), "rows", split_axis=0, concat_axis=0, tiled=True)
        )

    def return_terms(term_rows):
        outgoing = jnp.einsum("rs,rf->sf", to_slot, term_rows, precision=highest).reshape(
            row_count, capacity, term_rows.shape[1]
        )
        incoming = lax.all_to_all(outgoing, "rows", split_axis=0, concat_axis=0, tiled=True)
        return jnp.einsum(
            "sb,sf->bf", picked, incoming.reshape(slot_count, term_rows.shape[1]), precision=highest
        )

    incoming = (
        lax.all_to_all(select_rows(coord_rows), "rows", split_axis=0, concat_axis=0, tiled=True),
        lax.all_to_all(select_rows(observations), "rows", split_axis=0, concat_axis=0, tiled=True),
    )
    near_coords = to_refs(incoming[0])
    near_values = to_refs(incoming[1])
    near_points = near_coords.reshape(blocks, 3, 3, block_size)
    near_obs = near_values.reshape(blocks, 3, block_size)
    point_sets = jnp.concatenate([jnp.swapaxes(near_points, 1, 2), points[:, :, None]], axis=2)
    value_sets = jnp.concatenate([near_obs, observations[:, None]], axis=1)
    per_device = blocks // lax.axis_size("probe")
    first_block = lax.axis_index("probe") * per_device
    conditioner, whitened, block_terms = factor_blocks(
        lax.dynamic_slice_in_dim(
            point_sets.reshape(blocks, 3, 4 * block_size), first_block, per_device, 0
        ),
        lax.dynamic_slice_in_dim(
            value_sets.reshape(blocks, 4 * block_size), first_block, per_device, 0
        ),
    )
    conditioner, whitened, block_terms = (
        lax.all_gather(conditioner, "probe", axis=0, tiled=True),
        lax.all_gather(whitened, "probe", axis=0, tiled=True),
        lax.all_gather(block_terms, "probe", axis=0, tiled=True),
    )
    cond_four = conditioner.reshape(blocks, block_size, 4, block_size)

    def apply_operator(vector):
        near_vec = fetch_rows(vector.reshape(blocks, probe_cols * block_size)).reshape(
            blocks, 3, probe_cols, block_size
        )
        stacked = jnp.concatenate([near_vec, vector[:, None]], axis=1)
        projected = jnp.einsum("bjpm,bkjm->bpk", stacked, cond_four, precision=highest)
        spread = jnp.einsum("bpk,bkjm->bjpm", projected, cond_four, precision=highest)
        returned = return_terms(spread[:, :3].reshape(references, probe_cols * block_size))
        return spread[:, 3] + returned.reshape(blocks, probe_cols, block_size)

    square_sum = lax.psum(local_inner(probes, probes), "rows")
    probe_scale = jnp.sqrt(square_sum / cells + epsilon)
    basis_one = probes / probe_scale[None, :, None]
    image_one = apply_operator(basis_one)
    alpha_one = lax.psum(local_inner(basis_one, image_one), "rows") / cells
    residue = image_one - alpha_one[None, :, None] * basis_one
    beta_one = jnp.sqrt(lax.psum(local_inner(residue, residue), "rows") / cells + epsilon)
    basis_two = residue / beta_one[None, :, None]
    image_two = apply_operator(basis_two)
    alpha_two = lax.psum(local_inner(basis_two, image_two), "rows") / cells
    remainder = (
        image_two - alpha_two[None, :, None] * basis_two - beta_one[None, :, None] * basis_one
    )
    tridiagonal = jnp.stack([alpha_one, beta_one, alpha_two], axis=1)
    return (whitened, block_terms, tridiagonal, remainder)


def solution(mesh):
    placed = (
        P("rows", None, None),
        P("rows", None),
        P("rows", "probe", None),
        P("rows", None),
        P("rows"),
    )
    return jax.shard_map(
        body,
        mesh=mesh,
        in_specs=placed,
        out_specs=(P("rows", None), P("rows"), P("probe", None), P("rows", "probe", None)),
        check_vma=False,
    )
```

```python
import functools
import math

import jax
import jax.numpy as jnp
from jax import lax
from jax.experimental import pallas as pl
from jax.experimental.pallas import tpu as pltpu
from jax.sharding import PartitionSpec as P

length_scale = 0.3
nugget = 0.25
epsilon = 1e-06
highest = lax.Precision.HIGHEST
chunk = 8
width = 4


def dot(left, right):
    return jnp.dot(left, right, precision=highest, preferred_element_type=jnp.float32)


def dot_nt(left, right):
    return lax.dot_general(
        left, right, (((1,), (1,)), ((), ())), precision=highest,
        preferred_element_type=jnp.float32,
    )


def pivot_inverse(rows, e):
    rows = list(rows)
    e = [list(r) for r in e]
    for k in range(width):
        inv = 1.0 / e[k][k]
        rows[k] = rows[k] * inv
        for n in range(k + 1, width):
            e[k][n] = e[k][n] * inv
        for m in range(width):
            if m != k:
                f = e[m][k]
                rows[m] = rows[m] - f * rows[k]
                for n in range(k + 1, width):
                    e[m][n] = e[m][n] - f * e[k][n]
    return rows


def pivot_factor(rows, e):
    e = [list(r) for r in e]
    y = list(rows)
    inv = []
    product = None
    for k in range(width):
        d = e[k][k]
        s = lax.rsqrt(d)
        s = s * (1.5 - 0.5 * d * s * s)
        inv.append(s)
        product = s if product is None else product * s
        y[k] = y[k] * s
        for m in range(k + 1, width):
            e[m][k] = e[m][k] * s
        for m in range(k + 1, width):
            y[m] = y[m] - e[m][k] * y[k]
            for n in range(k + 1, m + 1):
                e[m][n] = e[m][n] - e[m][k] * e[n][k]
    r = list(y)
    for k in reversed(range(width)):
        for m in range(k + 1, width):
            r[k] = r[k] - e[m][k] * r[m]
        r[k] = r[k] * inv[k]
    return y, r, jnp.log(product)


def sweep(mats, factor):
    count = len(mats[0])
    shape = mats[0][0].shape
    lane = lax.broadcasted_iota(jnp.int32, shape, 1)
    sub = lax.broadcasted_iota(jnp.int32, shape, 0)

    def full(x):
        return jnp.broadcast_to(x, shape)

    def step(t, carry):
        mats, logs = carry
        mats = [list(m) for m in mats]
        logs = list(logs)
        for o in range(0, chunk, width):
            picked = (lane >= o) & (lane < o + width)
            for b in range(len(mats)):
                chunks = mats[b]
                top = chunks[0]
                cols = [full(top[:, o + k : o + k + 1]) for k in range(width)]
                rows = [full(top[o + k : o + k + 1, :]) for k in range(width)]
                e = [[full(cols[k][o + m : o + m + 1, :]) for k in range(width)] for m in range(width)]
                rows = [
                    jnp.where(lane == o + k, 1.0, jnp.where(picked, 0.0, rows[k]))
                    for k in range(width)
                ]
                if factor:
                    kept, r, term = pivot_factor(rows, e)
                    logs[b] = logs[b] + term
                else:
                    r = pivot_inverse(rows, e)
                    kept = r
                for p in range(count):
                    old = chunks[p]
                    if p:
                        cols = [full(old[:, o + k : o + k + 1]) for k in range(width)]
                    new = jnp.where(picked, 0.0, old)
                    for k in range(width):
                        new = new - cols[k] * r[k]
                    if p == 0:
                        if factor:
                            new = jnp.where(sub >= o + width, new, old)
                        for k in range(width):
                            new = jnp.where(sub == o + k, kept[k], new)
                    elif factor:
                        new = jnp.where(t + p < count, new, old)
                    chunks[p] = new
        turned = []
        for chunks in mats:
            chunks = [pltpu.roll(c, shape[1] - chunk, 1) for c in chunks]
            turned.append(tuple(chunks[1:] + chunks[:1]))
        return tuple(turned), tuple(logs)

    zero = jnp.zeros(shape, jnp.float32)
    return lax.fori_loop(0, count, step, (mats, tuple(zero for _ in mats)))


MESH = pl.DeviceIdType.MESH


def to_peers(axis, count, source, target, send_sem, recv_sem):
    me = lax.axis_index(axis)
    copies = []
    for p in range(1, count):
        peer = lax.rem(me + p, count)
        copies.append(
            pltpu.make_async_remote_copy(
                src_ref=source(peer),
                dst_ref=target,
                send_sem=send_sem.at[p - 1],
                recv_sem=recv_sem.at[p - 1],
                device_id={axis: peer},
                device_id_type=MESH,
            )
        )
    for copy in copies:
        copy.start()
    return copies


def wait_all(copies):
    for copy in copies:
        copy.wait()


def greet(counts):
    barrier = pltpu.get_barrier_semaphore()
    total = 0
    for axis, count in counts:
        for p in range(1, count):
            peer = lax.rem(lax.axis_index(axis) + p, count)
            pl.semaphore_signal(barrier, inc=1, device_id={axis: peer}, device_id_type=MESH)
            total += 1
    pl.semaphore_wait(barrier, total)


def gather_kernel(count, *refs):
    half = 4
    sources, targets, (send_sem, recv_sem, own_sem) = refs[:half], refs[half : 2 * half], refs[2 * half :]
    me = lax.axis_index("rows")
    greet((("rows", count),))
    copies = []
    for i in range(half):
        copies += to_peers(
            "rows", count, lambda peer: sources[i], targets[i].at[me], send_sem.at[i], recv_sem.at[i]
        )
    owns = [
        pltpu.make_async_copy(sources[i], targets[i].at[me], own_sem.at[i]) for i in range(half)
    ]
    for own in owns:
        own.start()
    for own in owns:
        own.wait()
    wait_all(copies)


def gather_rows(count, arrays):
    vmem = pl.BlockSpec(memory_space=pltpu.VMEM)
    return pl.pallas_call(
        functools.partial(gather_kernel, count),
        out_shape=[jax.ShapeDtypeStruct((count,) + a.shape, a.dtype) for a in arrays],
        in_specs=[vmem] * len(arrays),
        out_specs=[vmem] * len(arrays),
        scratch_shapes=[
            pltpu.SemaphoreType.DMA((len(arrays), count - 1)),
            pltpu.SemaphoreType.DMA((len(arrays), count - 1)),
            pltpu.SemaphoreType.DMA((len(arrays),)),
        ],
        compiler_params=pltpu.CompilerParams(collective_id=0, has_side_effects=True),
    )(*arrays)


def factor_kernel(
    capacity, share, first_ref, near_ref, pos_ref, points_ref, values_ref,
    g_ref, slot_ref, recv_ref, a_ref, seen_ref,
):
    nb = g_ref.shape[0]
    bs = points_ref.shape[3]
    count, blocks = points_ref.shape[:2]
    me = first_ref[0]
    first = first_ref[1]

    def position(owner, b, j):
        ident = near_ref[owner, b, j]
        return pos_ref[ident // blocks, 0, ident % blocks]

    def clear(i, c):
        slot_ref[i] = 3 * blocks
        recv_ref[i] = -1
        return c

    lax.fori_loop(0, count * capacity, clear, 0)

    def clear_seen(i, c):
        seen_ref[i] = 0
        return c

    lax.fori_loop(0, 2 * count, clear_seen, 0)

    def place_own(b, c):
        for j in range(3):
            at = position(me, b, j) // blocks
            rank = seen_ref[at]
            seen_ref[at] = rank + 1
            slot_ref[at * capacity + rank] = b * 3 + j
        return c

    lax.fori_loop(0, blocks, place_own, 0)

    def place(i, c):
        for j in range(3):
            sender = i // blocks
            row = position(sender, i % blocks, j)

            @pl.when(row // blocks == me)
            def _():
                rank = seen_ref[count + sender]
                seen_ref[count + sender] = rank + 1
                recv_ref[sender * capacity + rank] = row % blocks

        return c

    lax.fori_loop(0, count * blocks, place, 0)

    def part(i):
        return slice(i * bs, (i + 1) * bs)

    def load(j):
        return tuple(
            tuple(
                a_ref[b, j * bs + i * chunk : j * bs + (i + 1) * chunk, part(j)]
                for i in range(bs // chunk)
            )
            for b in range(nb)
        )

    same = lax.broadcasted_iota(jnp.int32, (bs, bs), 0) == lax.broadcasted_iota(
        jnp.int32, (bs, bs), 1
    )
    below = lax.broadcasted_iota(jnp.int32, (bs, bs), 0) >= lax.broadcasted_iota(
        jnp.int32, (bs, bs), 1
    )
    values = []
    for b in range(nb):
        at = [(position(me, first + b, j)) for j in range(3)]
        at = [(row // blocks, row % blocks) for row in at] + [(me, first + b)]
        rows = [points_ref[o, r] for o, r in at]
        values.append(
            jnp.concatenate(
                [jnp.broadcast_to(values_ref[o, pl.ds(r, 1)], (chunk, bs)) for o, r in at], axis=1
            )
        )
        pad = jnp.zeros((chunk - rows[0].shape[0], bs), jnp.float32)
        cols = [jnp.transpose(jnp.concatenate([row, pad], axis=0)) for row in rows]
        for i in range(4):
            for k in range(i + 1):
                dist_sq = None
                for c in range(3):
                    off = cols[i][:, c : c + 1] - rows[k][c : c + 1, :]
                    dist_sq = off * off if dist_sq is None else dist_sq + off * off
                value = 1.0 / (1.0 + dist_sq * (1.0 / (length_scale * length_scale)))
                if i == k:
                    value = value + jnp.where(same, nugget, 0.0)
                a_ref[b, part(i), part(k)] = value
    for j in range(3):
        inverse, _ = sweep(load(j), False)
        for b in range(nb):
            p = jnp.concatenate(inverse[b], axis=0)
            rest = a_ref[b, (j + 1) * bs :, part(j)]
            scaled = dot(rest, p)
            for i in range(j + 1, 4):
                row = scaled[(i - j - 1) * bs : (i - j) * bs]
                a_ref[b, part(i), (j + 1) * bs : (i + 1) * bs] -= dot_nt(
                    row, rest[: (i - j) * bs]
                )
            a_ref[b, (j + 1) * bs :, part(j)] = scaled
    low, logs = sweep(load(3), True)
    for b in range(nb):
        low_inv = jnp.where(below, jnp.concatenate(low[b], axis=0), 0.0)
        x2 = a_ref[b, part(3), part(2)]
        x1 = a_ref[b, part(3), part(1)] - dot(x2, a_ref[b, part(2), part(1)])
        x0 = (
            a_ref[b, part(3), part(0)]
            - dot(x1, a_ref[b, part(1), part(0)])
            - dot(x2, a_ref[b, part(2), part(0)])
        )
        g_ref[b, :bs, part(3)] = low_inv
        for i, x in enumerate((x0, x1, x2)):
            g_ref[b, :bs, part(i)] = -dot(low_inv, x)
        w = dot_nt(values[b], g_ref[b, :bs])
        square = jnp.sum(w[:1] * w[:1], axis=1, keepdims=True)
        term = (logs[b] - 0.5 * square) * (1.0 / bs) - 0.5 * math.log(2.0 * math.pi)
        g_ref[b, bs:, :] = jnp.concatenate([w, term, w, term], axis=1)


def factor_blocks(first, near, positions, points, values, nb, capacity):
    count, blocks, _, bs = points.shape
    smem = pl.BlockSpec(memory_space=pltpu.SMEM)
    vmem = pl.BlockSpec(memory_space=pltpu.VMEM)
    slots = jax.ShapeDtypeStruct((count * capacity,), jnp.int32)
    return pl.pallas_call(
        functools.partial(factor_kernel, capacity, nb),
        out_shape=(jax.ShapeDtypeStruct((nb, bs + chunk, 4 * bs), jnp.float32), slots, slots),
        in_specs=[smem, smem, smem, vmem, vmem],
        out_specs=(vmem, smem, smem),
        scratch_shapes=[
            pltpu.VMEM((nb, 4 * bs, 4 * bs), jnp.float32),
            pltpu.SMEM((2 * count,), jnp.int32),
        ],
        cost_estimate=pl.CostEstimate(
            flops=10**10, bytes_accessed=10**6, transcendentals=0
        ),
    )(first, near, positions, points, values)


def lanczos_kernel(
    count, depth, capacity, near_ref, pos_ref, slot_ref, recv_ref, g_ref, probes_ref,
    rem_ref, tri_ref, w_ref, t_ref,
    gall, q, z, sp, own, sb1, sb2, rb1, rb2,
    g_send, g_recv, r1_send, r1_recv, z_send, z_recv, r2_send, r2_recv, own_sem,
):
    me = lax.axis_index("rows")
    level = lax.axis_index("probe")
    total, cols, bs = probes_ref.shape
    blocks = total // count
    nb = g_ref.shape[0]
    cells = total * bs
    greet((("rows", count), ("probe", depth)))
    mine = gall.at[pl.ds(level * nb, nb)]
    g_copies = to_peers("probe", depth, lambda peer: g_ref, mine, g_send, g_recv)
    keep = pltpu.make_async_copy(g_ref, mine, own_sem)
    keep.start()

    def inner(f):
        acc = jnp.zeros((cols, bs), jnp.float32)
        for c in range(total):
            acc = acc + f(c)
        return jnp.sum(acc, axis=1, keepdims=True)

    scale = 1.0 / jnp.sqrt(inner(lambda c: probes_ref[c] * probes_ref[c]) / cells + epsilon)
    for c in range(total):
        q[c] = probes_ref[c] * scale
    sp[3 * blocks] = jnp.zeros((cols, bs), jnp.float32)
    keep.wait()
    wait_all(g_copies)
    for b in range(blocks):
        w_ref[b : b + 1] = gall[b, bs : bs + 1, :bs]
        t_ref[b : b + 1] = gall[b, bs : bs + 1, bs : 2 * bs]

    def apply_operator(source, sb, rb, send_sem, recv_sem):
        energy = jnp.zeros((cols, bs), jnp.float32)
        for b in range(blocks):
            parts = []
            for j in range(3):
                ident = near_ref[b, j]
                parts.append(source[pos_ref[ident // blocks, 0, ident % blocks]])
            parts.append(source[me * blocks + b])
            g = gall[b, :bs]
            projected = dot_nt(jnp.concatenate(parts, axis=1), g)
            energy = energy + projected * projected
            spread = dot(projected, g)
            for j in range(3):
                sp[b * 3 + j] = spread[:, j * bs : (j + 1) * bs]
            own[b] = spread[:, 3 * bs :]
        for d in range(count):
            for k in range(capacity):
                sb[d, k] = sp[slot_ref[d * capacity + k]]
            sb[d, capacity] = energy
        copies = to_peers("rows", count, lambda peer: sb.at[peer], rb.at[me], send_sem, recv_sem)
        rb[me] = sb[me]
        wait_all(copies)
        sums = [own[b] for b in range(blocks)]
        energy = jnp.zeros((cols, bs), jnp.float32)
        for d in range(count):
            for k in range(capacity):
                value = rb[d, k]
                local = recv_ref[d * capacity + k]
                for b in range(blocks):
                    sums[b] = sums[b] + jnp.where(local == b, value, 0.0)
            energy = energy + rb[d, capacity]
        return sums, jnp.sum(energy, axis=1, keepdims=True) / cells

    image, alpha_one = apply_operator(q, sb1, rb1, r1_send, r1_recv)
    for b in range(blocks):
        z[me * blocks + b] = image[b]
    here = z.at[pl.ds(me * blocks, blocks)]
    wait_all(to_peers("rows", count, lambda peer: here, here, z_send, z_recv))

    def residue(c):
        r = z[c] - alpha_one * q[c]
        return r * r

    beta_one = jnp.sqrt(inner(residue) / cells + epsilon)
    over = 1.0 / beta_one
    for b in range(blocks):
        own_q = q[me * blocks + b]
        rem_ref[b] = own_q
    for c in range(total):
        q[c] = (z[c] - alpha_one * q[c]) * over
    image, alpha_two = apply_operator(q, sb2, rb2, r2_send, r2_recv)
    for b in range(blocks):
        rem_ref[b] = image[b] - alpha_two * q[me * blocks + b] - beta_one * rem_ref[b]
    lane = lax.broadcasted_iota(jnp.int32, (cols, bs), 1)
    tri_ref[...] = jnp.where(lane == 0, alpha_one, jnp.where(lane == 1, beta_one, alpha_two))


def lanczos(count, depth, capacity, near, positions, slots, received, g, probes):
    total, cols, bs = probes.shape
    blocks = total // count
    smem = pl.BlockSpec(memory_space=pltpu.SMEM)
    vmem = pl.BlockSpec(memory_space=pltpu.VMEM)
    f32 = jnp.float32
    dma = pltpu.SemaphoreType.DMA
    exchange = pltpu.VMEM((count, capacity + 1, cols, bs), f32)
    return pl.pallas_call(
        functools.partial(lanczos_kernel, count, depth, capacity),
        out_shape=(
            jax.ShapeDtypeStruct((blocks, cols, bs), f32),
            jax.ShapeDtypeStruct((cols, bs), f32),
            jax.ShapeDtypeStruct((blocks, bs), f32),
            jax.ShapeDtypeStruct((blocks, bs), f32),
        ),
        in_specs=[smem] * 4 + [vmem] * 2,
        out_specs=(vmem,) * 4,
        scratch_shapes=[
            pltpu.VMEM((blocks,) + g.shape[1:], f32),
            pltpu.VMEM((total, cols, bs), f32),
            pltpu.VMEM((total, cols, bs), f32),
            pltpu.VMEM((3 * blocks + 1, cols, bs), f32),
            pltpu.VMEM((blocks, cols, bs), f32),
            exchange, exchange, exchange, exchange,
        ]
        + [dma((depth - 1,))] * 2
        + [dma((count - 1,))] * 6
        + [dma],
        compiler_params=pltpu.CompilerParams(collective_id=1, has_side_effects=True),
    )(near, positions, slots, received, g, probes)


def body(points, observations, probes, neighbours, block_position):
    count = lax.axis_size("rows")
    depth = lax.axis_size("probe")
    blocks = points.shape[0]
    capacity = max(2, 6 * blocks // count)
    nb = blocks // depth
    points_all, values_all, near_all, positions = gather_rows(
        count, (points, observations, neighbours, block_position.reshape(1, blocks))
    )
    probes_all = lax.all_gather(probes, "rows", axis=0, tiled=True)
    first = jnp.stack([lax.axis_index("rows"), lax.axis_index("probe") * nb]).astype(jnp.int32)
    g, slots, received = factor_blocks(
        first, near_all, positions, points_all, values_all, nb, capacity
    )
    remainder, tri, whitened, terms = lanczos(
        count, depth, capacity, neighbours, positions, slots, received, g, probes_all
    )
    return (whitened, terms[:, 0], tri[:, :3], remainder)


def solution(mesh):
    placed = (
        P("rows", None, None),
        P("rows", None),
        P("rows", "probe", None),
        P("rows", None),
        P("rows"),
    )
    return jax.shard_map(
        body,
        mesh=mesh,
        in_specs=placed,
        out_specs=(P("rows", None), P("rows"), P("probe", None), P("rows", "probe", None)),
        check_vma=False,
    )
```

```python
import functools
import math

import jax
import jax.numpy as jnp
from jax import lax
from jax.experimental import pallas as pl
from jax.experimental.pallas import tpu as pltpu
from jax.sharding import PartitionSpec as P

length_scale = 0.3
nugget = 0.25
epsilon = 1e-06
highest = lax.Precision.HIGHEST
chunk = 8
width = 4


def dot(left, right):
    return jnp.dot(left, right, precision=highest, preferred_element_type=jnp.float32)


def dot_nt(left, right):
    return lax.dot_general(
        left, right, (((1,), (1,)), ((), ())), precision=highest,
        preferred_element_type=jnp.float32,
    )


def pivot_inverse(rows, e):
    rows = list(rows)
    e = [list(r) for r in e]
    for k in range(width):
        inv = 1.0 / e[k][k]
        rows[k] = rows[k] * inv
        for n in range(k + 1, width):
            e[k][n] = e[k][n] * inv
        for m in range(width):
            if m != k:
                f = e[m][k]
                rows[m] = rows[m] - f * rows[k]
                for n in range(k + 1, width):
                    e[m][n] = e[m][n] - f * e[k][n]
    return rows


def pivot_factor(rows, e):
    e = [list(r) for r in e]
    y = list(rows)
    inv = []
    product = None
    for k in range(width):
        d = e[k][k]
        s = lax.rsqrt(d)
        s = s * (1.5 - 0.5 * d * s * s)
        inv.append(s)
        product = s if product is None else product * s
        y[k] = y[k] * s
        for m in range(k + 1, width):
            e[m][k] = e[m][k] * s
        for m in range(k + 1, width):
            y[m] = y[m] - e[m][k] * y[k]
            for n in range(k + 1, m + 1):
                e[m][n] = e[m][n] - e[m][k] * e[n][k]
    r = list(y)
    for k in reversed(range(width)):
        for m in range(k + 1, width):
            r[k] = r[k] - e[m][k] * r[m]
        r[k] = r[k] * inv[k]
    return y, r, jnp.log(product)


def sweep(mats, factor):
    count = len(mats[0])
    shape = mats[0][0].shape
    lane = lax.broadcasted_iota(jnp.int32, shape, 1)
    sub = lax.broadcasted_iota(jnp.int32, shape, 0)

    def full(x):
        return jnp.broadcast_to(x, shape)

    def step(t, carry):
        mats, logs = carry
        mats = [list(m) for m in mats]
        logs = list(logs)
        for o in range(0, chunk, width):
            picked = (lane >= o) & (lane < o + width)
            for b in range(len(mats)):
                chunks = mats[b]
                top = chunks[0]
                cols = [full(top[:, o + k : o + k + 1]) for k in range(width)]
                rows = [full(top[o + k : o + k + 1, :]) for k in range(width)]
                e = [[full(cols[k][o + m : o + m + 1, :]) for k in range(width)] for m in range(width)]
                rows = [
                    jnp.where(lane == o + k, 1.0, jnp.where(picked, 0.0, rows[k]))
                    for k in range(width)
                ]
                if factor:
                    kept, r, term = pivot_factor(rows, e)
                    logs[b] = logs[b] + term
                else:
                    r = pivot_inverse(rows, e)
                    kept = r
                for p in range(count):
                    old = chunks[p]
                    if p:
                        cols = [full(old[:, o + k : o + k + 1]) for k in range(width)]
                    new = jnp.where(picked, 0.0, old)
                    for k in range(width):
                        new = new - cols[k] * r[k]
                    if p == 0:
                        if factor:
                            new = jnp.where(sub >= o + width, new, old)
                        for k in range(width):
                            new = jnp.where(sub == o + k, kept[k], new)
                    elif factor:
                        new = jnp.where(t + p < count, new, old)
                    chunks[p] = new
        turned = []
        for chunks in mats:
            chunks = [pltpu.roll(c, shape[1] - chunk, 1) for c in chunks]
            turned.append(tuple(chunks[1:] + chunks[:1]))
        return tuple(turned), tuple(logs)

    zero = jnp.zeros(shape, jnp.float32)
    return lax.fori_loop(0, count, step, (mats, tuple(zero for _ in mats)))


MESH = pl.DeviceIdType.MESH


def to_peers(axis, count, source, target, send_sem, recv_sem):
    me = lax.axis_index(axis)
    copies = []
    for p in range(1, count):
        peer = lax.rem(me + p, count)
        copies.append(
            pltpu.make_async_remote_copy(
                src_ref=source(peer),
                dst_ref=target,
                send_sem=send_sem.at[p - 1],
                recv_sem=recv_sem.at[p - 1],
                device_id={axis: peer},
                device_id_type=MESH,
            )
        )
    for copy in copies:
        copy.start()
    return copies


def wait_all(copies):
    for copy in copies:
        copy.wait()


def greet(counts):
    barrier = pltpu.get_barrier_semaphore()
    total = 0
    for axis, count in counts:
        for p in range(1, count):
            peer = lax.rem(lax.axis_index(axis) + p, count)
            pl.semaphore_signal(barrier, inc=1, device_id={axis: peer}, device_id_type=MESH)
            total += 1
    pl.semaphore_wait(barrier, total)


def gather_kernel(count, *refs):
    half = 4
    sources, targets, (send_sem, recv_sem, own_sem) = refs[:half], refs[half : 2 * half], refs[2 * half :]
    me = lax.axis_index("rows")
    greet((("rows", count),))
    copies = []
    for i in range(half):
        copies += to_peers(
            "rows", count, lambda peer: sources[i], targets[i].at[me], send_sem.at[i], recv_sem.at[i]
        )
    owns = [
        pltpu.make_async_copy(sources[i], targets[i].at[me], own_sem.at[i]) for i in range(half)
    ]
    for own in owns:
        own.start()
    for own in owns:
        own.wait()
    wait_all(copies)


def gather_rows(count, arrays):
    vmem = pl.BlockSpec(memory_space=pltpu.VMEM)
    return pl.pallas_call(
        functools.partial(gather_kernel, count),
        out_shape=[jax.ShapeDtypeStruct((count,) + a.shape, a.dtype) for a in arrays],
        in_specs=[vmem] * len(arrays),
        out_specs=[vmem] * len(arrays),
        scratch_shapes=[
            pltpu.SemaphoreType.DMA((len(arrays), count - 1)),
            pltpu.SemaphoreType.DMA((len(arrays), count - 1)),
            pltpu.SemaphoreType.DMA((len(arrays),)),
        ],
        compiler_params=pltpu.CompilerParams(collective_id=0, has_side_effects=True),
    )(*arrays)


def plan_kernel(capacity, first_ref, near_ref, pos_ref, slot_ref, recv_ref, seen_ref):
    count, blocks = near_ref.shape[:2]
    me = first_ref[0]

    def position(owner, b, j):
        ident = near_ref[owner, b, j]
        return pos_ref[ident // blocks, 0, ident % blocks]

    for i in range(count * capacity):
        slot_ref[i] = 3 * blocks
        recv_ref[i] = -1
    for i in range(2 * count):
        seen_ref[i] = 0

    def place_own(b, c):
        for j in range(3):
            at = position(me, b, j) // blocks
            rank = seen_ref[at]
            seen_ref[at] = rank + 1
            slot_ref[at * capacity + rank] = b * 3 + j
        return c

    lax.fori_loop(0, blocks, place_own, 0)

    def place(i, c):
        for j in range(3):
            sender = i // blocks
            row = position(sender, i % blocks, j)

            @pl.when(row // blocks == me)
            def _():
                rank = seen_ref[count + sender]
                seen_ref[count + sender] = rank + 1
                recv_ref[sender * capacity + rank] = row % blocks

        return c

    lax.fori_loop(0, count * blocks, place, 0)


def plan_slots(first, near, positions, capacity):
    count = near.shape[0]
    smem = pl.BlockSpec(memory_space=pltpu.SMEM)
    slots = jax.ShapeDtypeStruct((count * capacity,), jnp.int32)
    return pl.pallas_call(
        functools.partial(plan_kernel, capacity),
        out_shape=(slots, slots),
        in_specs=[smem] * 3,
        out_specs=(smem, smem),
        scratch_shapes=[pltpu.SMEM((2 * count,), jnp.int32)],
    )(first, near, positions)


def build_kernels(near_rows, me, first, points_ref, a_ref):
    nb = a_ref.shape[0]
    blocks, _, bs = points_ref.shape[1:]

    def part(i):
        return slice(i * bs, (i + 1) * bs)

    same = lax.broadcasted_iota(jnp.int32, (bs, bs), 0) == lax.broadcasted_iota(
        jnp.int32, (bs, bs), 1
    )
    for b in range(nb):
        at = [(row // blocks, row % blocks) for row in near_rows[b]] + [(me, first + b)]
        rows = [points_ref[o, r] for o, r in at]
        pad = jnp.zeros((chunk - rows[0].shape[0], bs), jnp.float32)
        cols = [jnp.transpose(jnp.concatenate([row, pad], axis=0)) for row in rows]
        for i in range(4):
            for k in range(i + 1):
                dist_sq = None
                for c in range(3):
                    off = cols[i][:, c : c + 1] - rows[k][c : c + 1, :]
                    dist_sq = off * off if dist_sq is None else dist_sq + off * off
                value = 1.0 / (1.0 + dist_sq * (1.0 / (length_scale * length_scale)))
                if i == k:
                    value = value + jnp.where(same, nugget, 0.0)
                a_ref[b, part(i), part(k)] = value


def factor_blocks(near_rows, me, first, values_ref, a_ref, g_ref, wt_ref):
    nb, bs = g_ref.shape[:2]
    blocks = values_ref.shape[1]

    def part(i):
        return slice(i * bs, (i + 1) * bs)

    def load(j):
        return tuple(
            tuple(
                a_ref[b, j * bs + i * chunk : j * bs + (i + 1) * chunk, part(j)]
                for i in range(bs // chunk)
            )
            for b in range(nb)
        )

    below = lax.broadcasted_iota(jnp.int32, (bs, bs), 0) >= lax.broadcasted_iota(
        jnp.int32, (bs, bs), 1
    )
    for j in range(3):
        inverse, _ = sweep(load(j), False)
        for b in range(nb):
            p = jnp.concatenate(inverse[b], axis=0)
            rest = a_ref[b, (j + 1) * bs :, part(j)]
            scaled = dot(rest, p)
            for i in range(j + 1, 4):
                row = scaled[(i - j - 1) * bs : (i - j) * bs]
                a_ref[b, part(i), (j + 1) * bs : (i + 1) * bs] -= dot_nt(
                    row, rest[: (i - j) * bs]
                )
            a_ref[b, (j + 1) * bs :, part(j)] = scaled
    low, logs = sweep(load(3), True)
    for b in range(nb):
        low_inv = jnp.where(below, jnp.concatenate(low[b], axis=0), 0.0)
        x2 = a_ref[b, part(3), part(2)]
        x1 = a_ref[b, part(3), part(1)] - dot(x2, a_ref[b, part(2), part(1)])
        x0 = (
            a_ref[b, part(3), part(0)]
            - dot(x1, a_ref[b, part(1), part(0)])
            - dot(x2, a_ref[b, part(2), part(0)])
        )
        g_ref[b, :, part(3)] = low_inv
        for i, x in enumerate((x0, x1, x2)):
            g_ref[b, :, part(i)] = -dot(low_inv, x)
        at = [(row // blocks, row % blocks) for row in near_rows[b]] + [(me, first + b)]
        values = jnp.concatenate(
            [jnp.broadcast_to(values_ref[o, pl.ds(r, 1)], (chunk, bs)) for o, r in at], axis=1
        )
        w = dot_nt(values, g_ref[b])
        square = jnp.sum(w[:1] * w[:1], axis=1, keepdims=True)
        term = (logs[b] - 0.5 * square) * (1.0 / bs) - 0.5 * math.log(2.0 * math.pi)
        wt_ref[b] = jnp.concatenate([w, term], axis=1)


def main_kernel(
    count, depth, capacity,
    near_ref, pos_ref, slot_ref, recv_ref, points_ref, values_ref, probes_ref,
    rem_ref, tri_ref, w_ref, t_ref,
    a_ref, g_ref, wt_all, probes_all, q, z, sp,
    in1s, in1r, in2s, in2r, out1s, out1r, out2s, out2r, e1s, e1r, e2s, e2r,
    sb1, sb2, rb1, rb2, zsem, rsem, own_sem,
):
    me = lax.axis_index("rows")
    level = lax.axis_index("probe")
    blocks, cols, bs = probes_ref.shape
    total = blocks * count
    nb = g_ref.shape[0]
    cells = total * bs

    def position(b, j):
        ident = near_ref[me, b, j]
        return pos_ref[ident // blocks, 0, ident % blocks]

    def over_rows(i, source, target):
        return to_peers("rows", count, source, target, rsem.at[2 * i], rsem.at[2 * i + 1])

    def over_probe(i, source, target):
        return to_peers("probe", depth, source, target, zsem.at[2 * i], zsem.at[2 * i + 1])

    greet((("rows", count), ("probe", depth)))
    here = pl.ds(me * blocks, blocks)
    probe_copies = over_rows(0, lambda peer: probes_ref, probes_all.at[here])
    keep = pltpu.make_async_copy(probes_ref, probes_all.at[here], own_sem)
    keep.start()

    first = level * nb
    near_rows = [[position(first + b, j) for j in range(3)] for b in range(nb)]
    build_kernels(near_rows, me, first, points_ref, a_ref)

    def inner(f):
        acc = jnp.zeros((cols, bs), jnp.float32)
        for c in range(total):
            acc = acc + f(c)
        return jnp.sum(acc, axis=1, keepdims=True)

    def send_in(i, source, s, r):
        for b in range(blocks):
            parts = [source[position(b, j)] for j in range(3)] + [source[me * blocks + b]]
            s[b // nb, b % nb] = jnp.concatenate(parts, axis=1)
        copies = over_probe(i, lambda peer: s.at[peer], r.at[level])
        r[level] = s[level]
        return copies

    keep.wait()
    wait_all(probe_copies)
    scale = 1.0 / jnp.sqrt(inner(lambda c: probes_all[c] * probes_all[c]) / cells + epsilon)
    for c in range(total):
        q[c] = probes_all[c] * scale
    in_copies = send_in(0, q, in1s, in1r)
    sp[3 * blocks] = jnp.zeros((cols, bs), jnp.float32)
    factor_blocks(near_rows, me, first, values_ref, a_ref, g_ref, wt_all.at[level])
    wt_copies = over_probe(1, lambda peer: wt_all.at[level], wt_all.at[level])

    def apply_operator(i, inr, outs, outr, es, er, sb, rb):
        energy = jnp.zeros((depth * cols, bs), jnp.float32)
        for b in range(nb):
            stacked = jnp.concatenate([inr[d, b] for d in range(depth)], axis=0)
            projected = dot_nt(stacked, g_ref[b])
            energy = energy + projected * projected
            spread = dot(projected, g_ref[b])
            for d in range(depth):
                outs[d, b] = spread[d * cols : (d + 1) * cols]
        for d in range(depth):
            es[d] = energy[d * cols : (d + 1) * cols]
        copies = over_probe(2 * i, lambda peer: outs.at[peer], outr.at[level])
        copies += over_probe(2 * i + 1, lambda peer: es.at[peer], er.at[level])
        outr[level] = outs[level]
        er[level] = es[level]
        wait_all(copies)
        energy = er[0]
        for d in range(1, depth):
            energy = energy + er[d]
        for b in range(blocks):
            for j in range(3):
                sp[b * 3 + j] = outr[b // nb, b % nb, :, j * bs : (j + 1) * bs]
        for d in range(count):
            for k in range(capacity):
                sb[d, k] = sp[slot_ref[d * capacity + k]]
            sb[d, capacity] = energy
        copies = over_rows(i, lambda peer: sb.at[peer], rb.at[me])
        rb[me] = sb[me]
        wait_all(copies)
        sums = [outr[b // nb, b % nb, :, 3 * bs :] for b in range(blocks)]
        energy = jnp.zeros((cols, bs), jnp.float32)
        for d in range(count):
            for k in range(capacity):
                value = rb[d, k]
                local = recv_ref[d * capacity + k]
                for b in range(blocks):
                    sums[b] = sums[b] + jnp.where(local == b, value, 0.0)
            energy = energy + rb[d, capacity]
        return sums, jnp.sum(energy, axis=1, keepdims=True) / cells

    wait_all(in_copies)
    image, alpha_one = apply_operator(1, in1r, out1s, out1r, e1s, e1r, sb1, rb1)
    for b in range(blocks):
        z[me * blocks + b] = image[b]
    wait_all(over_rows(2, lambda peer: z.at[here], z.at[here]))

    def residue(c):
        r = z[c] - alpha_one * q[c]
        return r * r

    beta_one = jnp.sqrt(inner(residue) / cells + epsilon)
    over = 1.0 / beta_one
    for b in range(blocks):
        rem_ref[b] = q[me * blocks + b]
    for c in range(total):
        q[c] = (z[c] - alpha_one * q[c]) * over
    wait_all(send_in(4, q, in2s, in2r))
    image, alpha_two = apply_operator(3, in2r, out2s, out2r, e2s, e2r, sb2, rb2)
    for b in range(blocks):
        rem_ref[b] = image[b] - alpha_two * q[me * blocks + b] - beta_one * rem_ref[b]
    lane = lax.broadcasted_iota(jnp.int32, (cols, bs), 1)
    tri_ref[...] = jnp.where(lane == 0, alpha_one, jnp.where(lane == 1, beta_one, alpha_two))
    wait_all(wt_copies)
    for b in range(blocks):
        w_ref[b : b + 1] = wt_all[b // nb, b % nb, :1, :bs]
        t_ref[b : b + 1] = wt_all[b // nb, b % nb, :1, bs:]


def main_call(count, depth, capacity, near, positions, slots, received, points, values, probes):
    blocks, cols, bs = probes.shape
    total = blocks * count
    nb = blocks // depth
    smem = pl.BlockSpec(memory_space=pltpu.SMEM)
    vmem = pl.BlockSpec(memory_space=pltpu.VMEM)
    f32 = jnp.float32
    dma = pltpu.SemaphoreType.DMA
    wide = pltpu.VMEM((depth, nb, cols, 4 * bs), f32)
    small = pltpu.VMEM((depth, cols, bs), f32)
    exchange = pltpu.VMEM((count, capacity + 1, cols, bs), f32)
    return pl.pallas_call(
        functools.partial(main_kernel, count, depth, capacity),
        out_shape=(
            jax.ShapeDtypeStruct((blocks, cols, bs), f32),
            jax.ShapeDtypeStruct((cols, bs), f32),
            jax.ShapeDtypeStruct((blocks, bs), f32),
            jax.ShapeDtypeStruct((blocks, bs), f32),
        ),
        in_specs=[smem] * 4 + [vmem] * 3,
        out_specs=(vmem,) * 4,
        scratch_shapes=[
            pltpu.VMEM((nb, 4 * bs, 4 * bs), f32),
            pltpu.VMEM((nb, bs, 4 * bs), f32),
            pltpu.VMEM((depth, nb, chunk, 2 * bs), f32),
            pltpu.VMEM((total, cols, bs), f32),
            pltpu.VMEM((total, cols, bs), f32),
            pltpu.VMEM((total, cols, bs), f32),
            pltpu.VMEM((3 * blocks + 1, cols, bs), f32),
        ]
        + [wide] * 8
        + [small] * 4
        + [exchange] * 4
        + [dma((16, depth - 1)), dma((8, count - 1)), dma],
        compiler_params=pltpu.CompilerParams(collective_id=1, has_side_effects=True),
    )(near, positions, slots, received, points, values, probes)


def body(points, observations, probes, neighbours, block_position):
    count = lax.axis_size("rows")
    depth = lax.axis_size("probe")
    blocks = points.shape[0]
    capacity = max(2, 6 * blocks // count)
    points_all, values_all, near_all, positions = gather_rows(
        count, (points, observations, neighbours, block_position.reshape(1, blocks))
    )
    first = lax.axis_index("rows").astype(jnp.int32).reshape(1)
    slots, received = plan_slots(first, near_all, positions, capacity)
    remainder, tri, whitened, terms = main_call(
        count, depth, capacity, near_all, positions, slots, received,
        points_all, values_all, probes,
    )
    return (whitened, terms[:, 0], tri[:, :3], remainder)


def solution(mesh):
    placed = (
        P("rows", None, None),
        P("rows", None),
        P("rows", "probe", None),
        P("rows", None),
        P("rows"),
    )
    return jax.shard_map(
        body,
        mesh=mesh,
        in_specs=placed,
        out_specs=(P("rows", None), P("rows"), P("probe", None), P("rows", "probe", None)),
        check_vma=False,
    )
```

```python
import functools
import math

import jax
import jax.numpy as jnp
from jax import lax
from jax.experimental import pallas as pl
from jax.experimental.pallas import tpu as pltpu
from jax.sharding import PartitionSpec as P

length_scale = 0.3
nugget = 0.25
epsilon = 1e-06
highest = lax.Precision.HIGHEST
chunk = 8
width = 4


def dot(left, right):
    return jnp.dot(left, right, precision=highest, preferred_element_type=jnp.float32)


def dot_nt(left, right):
    return lax.dot_general(
        left, right, (((1,), (1,)), ((), ())), precision=highest,
        preferred_element_type=jnp.float32,
    )


def pivot_factor(rows, e):
    e = [list(r) for r in e]
    y = list(rows)
    inv = []
    product = None
    for k in range(width):
        d = e[k][k]
        s = lax.rsqrt(d)
        s = s * (1.5 - 0.5 * d * s * s)
        inv.append(s)
        product = s if product is None else product * s
        y[k] = y[k] * s
        for m in range(k + 1, width):
            e[m][k] = e[m][k] * s
        for m in range(k + 1, width):
            y[m] = y[m] - e[m][k] * y[k]
            for n in range(k + 1, m + 1):
                e[m][n] = e[m][n] - e[m][k] * e[n][k]
    r = list(y)
    for k in reversed(range(width)):
        for m in range(k + 1, width):
            r[k] = r[k] - e[m][k] * r[m]
        r[k] = r[k] * inv[k]
    return y, r, jnp.log(product)


def sweep(mats):
    count = len(mats[0])
    shape = mats[0][0].shape
    lane = lax.broadcasted_iota(jnp.int32, shape, 1)
    sub = lax.broadcasted_iota(jnp.int32, shape, 0)
    segment = max(1, count // 4)

    def full(x):
        return jnp.broadcast_to(x, shape)

    def step(start, t, carry):
        mats, logs = carry
        mats = [list(m) for m in mats]
        logs = list(logs)
        for o in range(0, chunk, width):
            picked = (lane >= o) & (lane < o + width)
            for b in range(len(mats)):
                chunks = mats[b]
                top = chunks[0]
                cols = [full(top[:, o + k : o + k + 1]) for k in range(width)]
                rows = [full(top[o + k : o + k + 1, :]) for k in range(width)]
                e = [[full(cols[k][o + m : o + m + 1, :]) for k in range(width)] for m in range(width)]
                rows = [
                    jnp.where(lane == o + k, 1.0, jnp.where(picked, 0.0, rows[k]))
                    for k in range(width)
                ]
                kept, r, term = pivot_factor(rows, e)
                logs[b] = logs[b] + term
                for p in range(count - start):
                    old = chunks[p]
                    if p == 0 and o + width == chunk:
                        new = old
                    else:
                        if p:
                            cols = [full(old[:, o + k : o + k + 1]) for k in range(width)]
                        new = jnp.where(picked, 0.0, old)
                        for k in range(width):
                            new = new - cols[k] * r[k]
                    if p == 0:
                        new = jnp.where(sub >= o + width, new, old)
                        for k in range(width):
                            new = jnp.where(sub == o + k, kept[k], new)
                    elif p > count - start - segment:
                        new = jnp.where(t + p < count, new, old)
                    chunks[p] = new
        turned = []
        for chunks in mats:
            chunks = [pltpu.roll(c, shape[1] - chunk, 1) for c in chunks]
            turned.append(tuple(chunks[1:] + chunks[:1]))
        return tuple(turned), tuple(logs)

    zero = jnp.zeros(shape, jnp.float32)
    carry = (mats, tuple(zero for _ in mats))
    for start in range(0, count, segment):
        carry = lax.fori_loop(start, start + segment, functools.partial(step, start), carry)
    return carry


MESH = pl.DeviceIdType.MESH


def to_peers(axis, count, source, target, send_sem, recv_sem):
    me = lax.axis_index(axis)
    copies = []
    for p in range(1, count):
        peer = lax.rem(me + p, count)
        copies.append(
            pltpu.make_async_remote_copy(
                src_ref=source(peer),
                dst_ref=target,
                send_sem=send_sem.at[p - 1],
                recv_sem=recv_sem.at[p - 1],
                device_id={axis: peer},
                device_id_type=MESH,
            )
        )
    for copy in copies:
        copy.start()
    return copies


def wait_all(copies):
    for copy in copies:
        copy.wait()


def greet(counts):
    barrier = pltpu.get_barrier_semaphore()
    total = 0
    for axis, count in counts:
        for p in range(1, count):
            peer = lax.rem(lax.axis_index(axis) + p, count)
            pl.semaphore_signal(barrier, inc=1, device_id={axis: peer}, device_id_type=MESH)
            total += 1
    pl.semaphore_wait(barrier, total)


def gather_kernel(count, *refs):
    half = 4
    sources, targets, (send_sem, recv_sem, own_sem) = refs[:half], refs[half : 2 * half], refs[2 * half :]
    me = lax.axis_index("rows")
    greet((("rows", count),))
    copies = []
    for i in range(half):
        copies += to_peers(
            "rows", count, lambda peer: sources[i], targets[i].at[me], send_sem.at[i], recv_sem.at[i]
        )
    owns = [
        pltpu.make_async_copy(sources[i], targets[i].at[me], own_sem.at[i]) for i in range(half)
    ]
    for own in owns:
        own.start()
    for own in owns:
        own.wait()
    wait_all(copies)


def gather_rows(count, arrays):
    vmem = pl.BlockSpec(memory_space=pltpu.VMEM)
    return pl.pallas_call(
        functools.partial(gather_kernel, count),
        out_shape=[jax.ShapeDtypeStruct((count,) + a.shape, a.dtype) for a in arrays],
        in_specs=[vmem] * len(arrays),
        out_specs=[vmem] * len(arrays),
        scratch_shapes=[
            pltpu.SemaphoreType.DMA((len(arrays), count - 1)),
            pltpu.SemaphoreType.DMA((len(arrays), count - 1)),
            pltpu.SemaphoreType.DMA((len(arrays),)),
        ],
        compiler_params=pltpu.CompilerParams(collective_id=0, has_side_effects=True),
    )(*arrays)


def plan_kernel(capacity, first_ref, near_ref, pos_ref, slot_ref, local_ref, seen_ref):
    count, blocks = near_ref.shape[:2]
    me = first_ref[0]

    def position(owner, b, j):
        ident = near_ref[owner, b, j]
        return pos_ref[ident // blocks, 0, ident % blocks]

    for i in range(count * capacity):
        slot_ref[i] = 3 * blocks
        local_ref[i] = -1
    for i in range(count):
        seen_ref[i] = 0

    def place_own(b, c):
        for j in range(3):
            row = position(me, b, j)
            at = row // blocks
            rank = seen_ref[at]
            seen_ref[at] = rank + 1
            slot_ref[at * capacity + rank] = b * 3 + j
            local_ref[at * capacity + rank] = row % blocks
        return c

    lax.fori_loop(0, blocks, place_own, 0)


def plan_slots(first, near, positions, capacity):
    count = near.shape[0]
    smem = pl.BlockSpec(memory_space=pltpu.SMEM)
    slots = jax.ShapeDtypeStruct((count * capacity,), jnp.int32)
    return pl.pallas_call(
        functools.partial(plan_kernel, capacity),
        out_shape=(slots, slots),
        in_specs=[smem] * 3,
        out_specs=(smem, smem),
        scratch_shapes=[pltpu.SMEM((count,), jnp.int32)],
    )(first, near, positions)


def build_kernels(near_rows, me, first, points_ref, a_ref):
    nb = a_ref.shape[0]
    blocks, _, bs = points_ref.shape[1:]

    def part(i):
        return slice(i * bs, (i + 1) * bs)

    same = lax.broadcasted_iota(jnp.int32, (bs, bs), 0) == lax.broadcasted_iota(
        jnp.int32, (bs, bs), 1
    )
    for b in range(nb):
        at = [(row // blocks, row % blocks) for row in near_rows[b]] + [(me, first + b)]
        rows = [points_ref[o, r] for o, r in at]
        pad = jnp.zeros((chunk - rows[0].shape[0], bs), jnp.float32)
        cols = [jnp.transpose(jnp.concatenate([row, pad], axis=0)) for row in rows]
        for i in range(4):
            for k in range(i + 1):
                dist_sq = None
                for c in range(3):
                    off = cols[i][:, c : c + 1] - rows[k][c : c + 1, :]
                    dist_sq = off * off if dist_sq is None else dist_sq + off * off
                value = 1.0 / (1.0 + dist_sq * (1.0 / (length_scale * length_scale)))
                if i == k:
                    value = value + jnp.where(same, nugget, 0.0)
                a_ref[b, part(i), part(k)] = value


def factor_blocks(near_rows, me, first, values_ref, a_ref, g_ref, wt_ref):
    nb, bs = g_ref.shape[:2]
    blocks = values_ref.shape[1]

    def part(i):
        return slice(i * bs, (i + 1) * bs)

    def load(j):
        return tuple(
            tuple(
                a_ref[b, j * bs + i * chunk : j * bs + (i + 1) * chunk, part(j)]
                for i in range(bs // chunk)
            )
            for b in range(nb)
        )

    below = lax.broadcasted_iota(jnp.int32, (bs, bs), 0) >= lax.broadcasted_iota(
        jnp.int32, (bs, bs), 1
    )
    invs = []
    for j in range(4):
        low, logs = sweep(load(j))
        invs.append([jnp.where(below, jnp.concatenate(low[b], axis=0), 0.0) for b in range(nb)])
        if j == 3:
            break
        for b in range(nb):
            scaled = dot_nt(a_ref[b, (j + 1) * bs :, part(j)], invs[j][b])
            for i in range(j + 1, 4):
                row = scaled[(i - j - 1) * bs : (i - j) * bs]
                a_ref[b, part(i), (j + 1) * bs : (i + 1) * bs] -= dot_nt(
                    row, scaled[: (i - j) * bs]
                )
            a_ref[b, (j + 1) * bs :, part(j)] = scaled
            a_ref[b, part(j), part(j)] = invs[j][b]
    for b in range(nb):
        low_inv = invs[3][b]
        x2 = dot(a_ref[b, part(3), part(2)], a_ref[b, part(2), part(2)])
        x1 = dot(
            a_ref[b, part(3), part(1)] - dot(x2, a_ref[b, part(2), part(1)]),
            a_ref[b, part(1), part(1)],
        )
        x0 = dot(
            a_ref[b, part(3), part(0)]
            - dot(x1, a_ref[b, part(1), part(0)])
            - dot(x2, a_ref[b, part(2), part(0)]),
            a_ref[b, part(0), part(0)],
        )
        g_ref[b, :, part(3)] = low_inv
        for i, x in enumerate((x0, x1, x2)):
            g_ref[b, :, part(i)] = -dot(low_inv, x)
        at = [(row // blocks, row % blocks) for row in near_rows[b]] + [(me, first + b)]
        values = jnp.concatenate(
            [jnp.broadcast_to(values_ref[o, pl.ds(r, 1)], (chunk, bs)) for o, r in at], axis=1
        )
        w = dot_nt(values, g_ref[b])
        square = jnp.sum(w[:1] * w[:1], axis=1, keepdims=True)
        term = (logs[b] - 0.5 * square) * (1.0 / bs) - 0.5 * math.log(2.0 * math.pi)
        wt_ref[b] = jnp.concatenate([w, term], axis=1)


def main_kernel(
    count, depth, capacity,
    near_ref, pos_ref, slot_ref, local_ref, points_ref, values_ref, probes_ref,
    rem_ref, tri_ref, w_ref, t_ref,
    a_ref, g_ref, wt_all, probes_all, q, z, sp,
    in1s, in1r, in2s, in2r, out1s, out1r, out2s, out2r, e1s, e1r, e2s, e2r,
    sb1, sb2, rb1, rb2, zsem, rsem, own_sem,
):
    me = lax.axis_index("rows")
    level = lax.axis_index("probe")
    blocks, cols, bs = probes_ref.shape
    total = blocks * count
    nb = g_ref.shape[0]
    cells = total * bs

    def position(b, j):
        ident = near_ref[me, b, j]
        return pos_ref[ident // blocks, 0, ident % blocks]

    def over_rows(i, source, target):
        return to_peers("rows", count, source, target, rsem.at[2 * i], rsem.at[2 * i + 1])

    def over_probe(i, source, target):
        return to_peers("probe", depth, source, target, zsem.at[2 * i], zsem.at[2 * i + 1])

    greet((("rows", count), ("probe", depth)))
    line = lax.broadcasted_iota(jnp.int32, (cols, bs), 0)
    here = pl.ds(me * blocks, blocks)
    probe_copies = over_rows(0, lambda peer: probes_ref, probes_all.at[here])
    keep = pltpu.make_async_copy(probes_ref, probes_all.at[here], own_sem)
    keep.start()

    first = level * nb
    near_rows = [[position(first + b, j) for j in range(3)] for b in range(nb)]
    build_kernels(near_rows, me, first, points_ref, a_ref)

    def inner(f):
        acc = jnp.zeros((cols, bs), jnp.float32)
        for c in range(total):
            acc = acc + f(c)
        return jnp.sum(acc, axis=1, keepdims=True)

    def send_in(i, source, s, r):
        for b in range(blocks):
            parts = [source[position(b, j)] for j in range(3)] + [source[me * blocks + b]]
            s[b // nb, b % nb] = jnp.concatenate(parts, axis=1)
        copies = over_probe(i, lambda peer: s.at[peer], r.at[level])
        r[level] = s[level]
        return copies

    keep.wait()
    wait_all(probe_copies)
    scale = 1.0 / jnp.sqrt(inner(lambda c: probes_all[c] * probes_all[c]) / cells + epsilon)
    for c in range(total):
        q[c] = probes_all[c] * scale
    in_copies = send_in(0, q, in1s, in1r)
    sp[3 * blocks] = jnp.zeros((cols, bs), jnp.float32)
    factor_blocks(near_rows, me, first, values_ref, a_ref, g_ref, wt_all.at[level])
    wt_copies = over_probe(1, lambda peer: wt_all.at[level], wt_all.at[level])

    def apply_operator(i, inr, outs, outr, es, er, sb, rb):
        energy = jnp.zeros((depth * cols, bs), jnp.float32)
        for b in range(nb):
            stacked = jnp.concatenate([inr[d, b] for d in range(depth)], axis=0)
            projected = dot_nt(stacked, g_ref[b])
            energy = energy + projected * projected
            spread = dot(projected, g_ref[b])
            for d in range(depth):
                outs[d, b] = spread[d * cols : (d + 1) * cols]
        for d in range(depth):
            es[d] = energy[d * cols : (d + 1) * cols]
        copies = over_probe(2 * i, lambda peer: outs.at[peer], outr.at[level])
        copies += over_probe(2 * i + 1, lambda peer: es.at[peer], er.at[level])
        outr[level] = outs[level]
        er[level] = es[level]
        wait_all(copies)
        energy = er[0]
        for d in range(1, depth):
            energy = energy + er[d]
        for b in range(blocks):
            for j in range(3):
                sp[b * 3 + j] = outr[b // nb, b % nb, :, j * bs : (j + 1) * bs]
        for d in range(count):
            for k in range(capacity):
                sb[d, k] = sp[slot_ref[d * capacity + k]]
            sb[d, capacity] = energy
            tile = jnp.full((cols, bs), -1, jnp.int32)
            for k in range(capacity):
                tile = jnp.where(line == k, local_ref[d * capacity + k], tile)
            sb[d, capacity + 1] = tile.astype(jnp.float32)
        copies = over_rows(i, lambda peer: sb.at[peer], rb.at[me])
        rb[me] = sb[me]
        wait_all(copies)
        sums = [outr[b // nb, b % nb, :, 3 * bs :] for b in range(blocks)]
        energy = jnp.zeros((cols, bs), jnp.float32)
        for d in range(count):
            tile = rb[d, capacity + 1]
            for k in range(capacity):
                value = rb[d, k]
                local = jnp.broadcast_to(tile[k : k + 1, :], (cols, bs))
                for b in range(blocks):
                    sums[b] = sums[b] + jnp.where(local == b, value, 0.0)
            energy = energy + rb[d, capacity]
        return sums, jnp.sum(energy, axis=1, keepdims=True) / cells

    wait_all(in_copies)
    image, alpha_one = apply_operator(1, in1r, out1s, out1r, e1s, e1r, sb1, rb1)
    for b in range(blocks):
        z[me * blocks + b] = image[b]
    wait_all(over_rows(2, lambda peer: z.at[here], z.at[here]))

    def residue(c):
        r = z[c] - alpha_one * q[c]
        return r * r

    beta_one = jnp.sqrt(inner(residue) / cells + epsilon)
    over = 1.0 / beta_one
    for b in range(blocks):
        rem_ref[b] = q[me * blocks + b]
    for c in range(total):
        q[c] = (z[c] - alpha_one * q[c]) * over
    wait_all(send_in(4, q, in2s, in2r))
    image, alpha_two = apply_operator(3, in2r, out2s, out2r, e2s, e2r, sb2, rb2)
    for b in range(blocks):
        rem_ref[b] = image[b] - alpha_two * q[me * blocks + b] - beta_one * rem_ref[b]
    lane = lax.broadcasted_iota(jnp.int32, (cols, bs), 1)
    tri_ref[...] = jnp.where(lane == 0, alpha_one, jnp.where(lane == 1, beta_one, alpha_two))
    wait_all(wt_copies)
    for b in range(blocks):
        w_ref[b : b + 1] = wt_all[b // nb, b % nb, :1, :bs]
        t_ref[b : b + 1] = wt_all[b // nb, b % nb, :1, bs:]


def main_call(count, depth, capacity, near, positions, slots, received, points, values, probes):
    blocks, cols, bs = probes.shape
    total = blocks * count
    nb = blocks // depth
    smem = pl.BlockSpec(memory_space=pltpu.SMEM)
    vmem = pl.BlockSpec(memory_space=pltpu.VMEM)
    f32 = jnp.float32
    dma = pltpu.SemaphoreType.DMA
    wide = pltpu.VMEM((depth, nb, cols, 4 * bs), f32)
    small = pltpu.VMEM((depth, cols, bs), f32)
    exchange = pltpu.VMEM((count, capacity + 2, cols, bs), f32)
    return pl.pallas_call(
        functools.partial(main_kernel, count, depth, capacity),
        out_shape=(
            jax.ShapeDtypeStruct((blocks, cols, bs), f32),
            jax.ShapeDtypeStruct((cols, bs), f32),
            jax.ShapeDtypeStruct((blocks, bs), f32),
            jax.ShapeDtypeStruct((blocks, bs), f32),
        ),
        in_specs=[smem] * 4 + [vmem] * 3,
        out_specs=(vmem,) * 4,
        scratch_shapes=[
            pltpu.VMEM((nb, 4 * bs, 4 * bs), f32),
            pltpu.VMEM((nb, bs, 4 * bs), f32),
            pltpu.VMEM((depth, nb, chunk, 2 * bs), f32),
            pltpu.VMEM((total, cols, bs), f32),
            pltpu.VMEM((total, cols, bs), f32),
            pltpu.VMEM((total, cols, bs), f32),
            pltpu.VMEM((3 * blocks + 1, cols, bs), f32),
        ]
        + [wide] * 8
        + [small] * 4
        + [exchange] * 4
        + [dma((16, depth - 1)), dma((8, count - 1)), dma],
        compiler_params=pltpu.CompilerParams(collective_id=1, has_side_effects=True),
    )(near, positions, slots, received, points, values, probes)


def body(points, observations, probes, neighbours, block_position):
    count = lax.axis_size("rows")
    depth = lax.axis_size("probe")
    blocks = points.shape[0]
    capacity = max(2, 6 * blocks // count)
    points_all, values_all, near_all, positions = gather_rows(
        count, (points, observations, neighbours, block_position.reshape(1, blocks))
    )
    first = lax.axis_index("rows").astype(jnp.int32).reshape(1)
    slots, received = plan_slots(first, near_all, positions, capacity)
    remainder, tri, whitened, terms = main_call(
        count, depth, capacity, near_all, positions, slots, received,
        points_all, values_all, probes,
    )
    return (whitened, terms[:, 0], tri[:, :3], remainder)


def solution(mesh):
    placed = (
        P("rows", None, None),
        P("rows", None),
        P("rows", "probe", None),
        P("rows", None),
        P("rows"),
    )
    return jax.shard_map(
        body,
        mesh=mesh,
        in_specs=placed,
        out_specs=(P("rows", None), P("rows"), P("probe", None), P("rows", "probe", None)),
        check_vma=False,
    )
```
